128 devices in a mesh: vv: 16 (over z, x), oo: 8 (over y, core).
Axes of the slice: x: 4, y: 4, z: 4, core: 2. Of those that a mesh axis runs over, the one named last changes fastest.
Arguments:
- integrals: bfloat16 [32768, 20480], P('vv', 'oo'), may hold values from -0.0390625 to 0.0390625
- t2: bfloat16 [8, 20480, 1280], P(None, 'oo', 'vv'), may hold values from -6 to 6
- block_owner: int32 [16], replicated, may hold values from 0 to 7, as said below
Outputs:
- residual: float32 [32768, 1280], P('vv', 'oo')
The draws below stay inside these ranges and needn't reach their ends.
Inputs may be any that keep to these rules, and one draw needn't show every extreme that they name: `block_owner`: each pair irrep 0 to 7 is named by exactly 2 row blocks.
All inputs are finite; a program needn't handle non-finite values.
Results may differ from the reference program's by a relative error of at most 0.0003.
Values may be sent and summed in bfloat16 or wider, within the bound.
A program may use at most 128 MiB of HBM per device.

```python
import jax
import jax.numpy as jnp
from jax import lax

G = 8
DE = 20480
IJ = 1280
ROW_DEV = 2048
OWNERS = 16
ROWS = 32768


def draw_block_owner(key, part):
    labels = jnp.arange(OWNERS, dtype=jnp.int32) % G
    return jax.random.permutation(key, labels).astype(jnp.int32)


def raised(entries, stream_key, source, target, shards_of, factor):
    def block_of(position):
        return (jnp.arange(entries.shape[position]) // (entries.shape[position] // shards_of)).reshape((-1,) + (1,) * (entries.ndim - 1 - position))

    first = jax.random.permutation(stream_key, shards_of)[block_of(target)]
    second = (block_of(target) + shards_of // 2) % shards_of
    return jnp.where((block_of(source) == first) | (block_of(source) == second), factor * entries, entries)


def steps_of(key, extent, cuts, smallest, high):
    loudness = 1.0
    for position, parts in cuts:
        heights = jax.random.uniform(jax.random.fold_in(jax.random.fold_in(key, 6), position), (parts,), jnp.float32, smallest / len(cuts), high / len(cuts))
        loudness = loudness * jnp.repeat(jnp.exp(heights), extent[position] // parts).reshape((-1,) + (1,) * (len(extent) - 1 - position))
    return loudness


def normal_values(key, extent, spread, most, shards=(), held_as=jnp.bfloat16):
    entries = jax.random.normal(key, extent, jnp.float32) * spread
    if len(shards) > 0:
        entries = steps_of(key, extent, shards, -0.22, 0.18) * entries
    return jnp.clip(entries, min=-most, max=most).astype(held_as)


def heavy_noise(stream_key, extent, deviation, reach, split, heavy, kind=jnp.bfloat16):
    entries = deviation * jax.random.normal(stream_key, extent, jnp.float32)
    if split:
        entries = entries * steps_of(stream_key, extent, split, -0.22, 0.18)
    return jnp.clip(raised(entries, jax.random.fold_in(stream_key, 3), *heavy), -reach, reach).astype(kind)


def setup_inputs(seed: int = 0) -> dict:
    seeds = jax.random.split(jax.random.key(seed), 4)
    return {
        "integrals": normal_values(seeds[0], (ROWS, DE), DE ** -0.5, 0.0390625, ((0, 16), (1, 8))),
        "t2": heavy_noise(seeds[1], (G, DE, IJ), 1.0, 6.0, ((1, 8), (2, 16)), (1, 2, 16, 2.0)),
        "block_owner": draw_block_owner(jax.random.fold_in(seeds[3], 71), 0),
    }


def reference(integrals, t2, block_owner):
    blocks = integrals.reshape(OWNERS, ROW_DEV, DE)

    def one_block(pair):
        rows, irrep = pair
        return jnp.dot(rows, t2[irrep], preferred_element_type=jnp.float32)

    result = lax.map(one_block, (blocks, block_owner))
    return result.reshape(OWNERS * ROW_DEV, IJ)
```

```python
import functools

import jax
import jax.numpy as jnp
from jax import lax
from jax.experimental import pallas as pl
from jax.experimental.pallas import tpu as pltpu
from jax.sharding import PartitionSpec as P

MESH = pl.DeviceIdType.MESH
ROUNDS = (16, 16, 16, 16, 16)
NCH = 4
RHS_T = (((1,), (1,)), ((), ()))


def wrap(i):
    return lax.rem(i, 4)


def kernel(rounds, owner, a_hbm, t_hbm, o_hbm, *scratch):
    R = len(rounds)
    scratch = list(scratch)

    def take(n):
        got = scratch[:n]
        del scratch[:n]
        return got

    (a,) = take(1)
    t2v, snd, arr, fin, ra, rb, part, xin, yr, yin, out = (take(R) for _ in range(11))
    a_sem, t_sem, o_sem, sA, rA, sB, rB, sX, rX, sY, rY = take(11)
    CH = a.shape[0] // NCH
    offs = [sum(rounds[:r]) for r in range(R)]

    v, o = lax.axis_index("vv"), lax.axis_index("oo")
    z, x, y, c = lax.div(v, 4), wrap(v), lax.div(o, 2), lax.rem(o, 2)
    f, s = z * (1 - c) + x * c, x * (1 - c) + z * c

    def plane(ff, ss):
        return ff * (4 - 3 * c) + ss * (1 + 3 * c)

    def dev_a(d):
        return (plane(wrap(f + d), s), o)

    def dev_b(d):
        return (plane(f, wrap(s + d)), o)

    def dev_y(d):
        return (v, wrap(y + d) * 2 + c)

    sibling = (v, y * 2 + 1 - c)

    def load_t(r):
        return pltpu.make_async_copy(t_hbm.at[:, pl.ds(offs[r], rounds[r]), :], t2v[r], t_sem.at[r])

    def load_a(i):
        rows = pl.ds(i * CH, CH)
        return pltpu.make_async_copy(a_hbm.at[rows], a.at[rows], a_sem.at[i])

    for r in range(R):
        load_t(r).start()
    for i in range(NCH):
        load_a(i).start()

    barrier = pltpu.get_barrier_semaphore()
    peers = [dev_a(1), dev_a(3), dev_b(1), dev_b(3), dev_y(1), dev_y(3), sibling]
    for peer in peers:
        pl.semaphore_signal(barrier, inc=1, device_id=peer, device_id_type=MESH)
    pl.semaphore_wait(barrier, len(peers))

    def send(src, dst, ss, rs, to):
        return pltpu.make_async_remote_copy(
            src_ref=src, dst_ref=dst, send_sem=ss, recv_sem=rs, device_id=to, device_id_type=MESH
        )

    def A(r, i):
        src, dst, d = [
            (snd[r].at[2, 0:2], ra[r].at[0], 1),
            (snd[r].at[2, 2:4], ra[r].at[1], 3),
            (snd[r].at[1], arr[r].at[1], 1),
            (snd[r].at[3], arr[r].at[3], 3),
            (ra[r].at[0], arr[r].at[2, 0:2], 1),
            (ra[r].at[1], arr[r].at[2, 2:4], 3),
        ][i]
        return send(src, dst, sA.at[r, i], rA.at[r, i], dev_a(d))

    def B(r, i):
        src, dst, d = [
            (snd[r].at[0, 2], rb[r].at[0, 0], 1),
            (snd[r].at[0, 1], fin[r].at[1, 0], 1),
            (snd[r].at[0, 3], fin[r].at[3, 0], 3),
            (arr[r].at[1, 2], rb[r].at[0, 1], 1),
            (arr[r].at[2:4, 2], rb[r].at[1], 3),
            (arr[r].at[1:4, 1], fin[r].at[1, 1:4], 1),
            (arr[r].at[1:4, 3], fin[r].at[3, 1:4], 3),
            (rb[r].at[0], fin[r].at[2, 0:2], 1),
            (rb[r].at[1], fin[r].at[2, 2:4], 3),
        ][i]
        return send(src, dst, sB.at[r, i], rB.at[r, i], dev_b(d))

    def X(r, ch):
        return send(part[r].at[ch, 1 - c], xin[r].at[ch], sX.at[r, ch], rX.at[r, ch], sibling)

    def Y(r, ch, i):
        src, dst, d = [
            (part[r].at[ch, c, wrap(y + 2), 0], yr[r].at[ch, 0], 1),
            (part[r].at[ch, c, wrap(y + 2), 1], yr[r].at[ch, 1], 3),
            (part[r].at[ch, c, wrap(y + 1)], yin[r].at[ch, 0], 1),
            (part[r].at[ch, c, wrap(y + 3)], yin[r].at[ch, 1], 3),
        ][i]
        return send(src, dst, sY.at[r, ch, i], rY.at[r, ch, i], dev_y(d))

    def prep(r):
        load_t(r).wait()
        for j in (2, 1, 3, 0):
            for t in range(4):
                block = t2v[r][owner[plane(wrap(f + j), wrap(s + t))]]
                if j == 0 and t == 0:
                    fin[r][0, 0] = block
                else:
                    snd[r][j, t] = block

    def multiply(r, ch):
        u = rounds[r]
        left = fin[r][...].reshape(16 * u, fin[r].shape[-1])
        rows = pl.ds(pl.multiple_of(ch * CH, CH), CH)
        res = lax.dot_general(left, a[rows, :], RHS_T, preferred_element_type=jnp.float32)
        for t in range(4):
            for j in range(4):
                ff, ss = wrap(f - j + 4), wrap(s - t + 4)
                zs, xs = ff * (1 - c) + ss * c, ss * (1 - c) + ff * c
                i = 4 * t + j
                part[r][ch, lax.div(xs, 2), zs, lax.rem(xs, 2)] = res[i * u : (i + 1) * u]
        X(r, ch).start()

    def chip_sum(r, ch):
        X(r, ch).wait_recv()
        part[r][ch, c] = part[r][ch, c] + xin[r][ch]
        Y(r, ch, 0).start()
        Y(r, ch, 1).start()

    def compute(r):
        for i in (1, 2, 5, 6, 7, 8):
            B(r, i).wait_recv()
        for j in (1, 2, 3):
            fin[r][0, j] = arr[r][j, 0]
        if r == 0:
            for i in range(NCH):
                load_a(i).wait()

        multiply(r, 0)

        @pl.loop(1, NCH)
        def _(ch):
            multiply(r, ch)
            chip_sum(r, ch - 1)

        chip_sum(r, NCH - 1)

    def relay_y(r):
        @pl.loop(0, NCH)
        def _(ch):
            for i in range(2):
                d = wrap(y + 1 + 2 * i)
                Y(r, ch, i).wait_recv()
                part[r][ch, c, d, i] = part[r][ch, c, d, i] + yr[r][ch, i]
                Y(r, ch, 2 + i).start()

    def store(r, h):
        return pltpu.make_async_copy(out[r].at[h], o_hbm.at[pl.ds(80 * h + offs[r], rounds[r]), :], o_sem.at[r, h])

    def finish(r):
        @pl.loop(0, NCH)
        def _(ch):
            Y(r, ch, 2).wait_recv()
            Y(r, ch, 3).wait_recv()
            cols = pl.ds(pl.multiple_of(ch * CH, CH), CH)
            out[r][:, :, cols] = part[r][ch, c, y] + yin[r][ch, 0] + yin[r][ch, 1]

        for h in range(2):
            store(r, h).start()

    prep(0)
    for k in range(-1, R + 3):
        if k + 1 < R:
            for i in range(4):
                A(k + 1, i).start()
            for i in range(3):
                B(k + 1, i).start()
        if k + 2 < R:
            prep(k + 2)
        if 0 <= k < R:
            for i in (2, 3, 4, 5):
                A(k, i).wait_recv()
            for i in (3, 4, 5, 6):
                B(k, i).start()
        if k + 1 < R:
            for i in range(2):
                A(k + 1, i).wait_recv()
                A(k + 1, 4 + i).start()
        if 0 <= k - 2 < R:
            relay_y(k - 2)
        if 0 <= k < R:
            B(k, 0).wait_recv()
            B(k, 3).wait_recv()
            B(k, 7).start()
            B(k, 4).wait_recv()
            B(k, 8).start()
        if 0 <= k - 3 < R:
            finish(k - 3)
        if 0 <= k - 1 < R:
            compute(k - 1)

    for r in range(R):
        for i in range(6):
            A(r, i).wait_send()
        for i in range(9):
            B(r, i).wait_send()
        for h in range(2):
            store(r, h).wait()

        @pl.loop(0, NCH)
        def _(ch):
            X(r, ch).wait_send()
            for i in range(4):
                Y(r, ch, i).wait_send()


def local(integrals, t2, block_owner):
    t2 = jnp.swapaxes(t2, 1, 2)
    groups, width, depth = t2.shape
    rows = integrals.shape[0]
    R, ch = len(ROUNDS), rows // NCH
    bf16, f32 = jnp.bfloat16, jnp.float32

    def each(shape, dtype):
        return [pltpu.VMEM(shape(u), dtype) for u in ROUNDS]

    scratch = (
        [pltpu.VMEM((rows, depth), bf16)]
        + each(lambda u: (groups, u, depth), bf16)
        + each(lambda u: (4, 4, u, depth), bf16)
        + each(lambda u: (4, 4, u, depth), bf16)
        + each(lambda u: (4, 4, u, depth), bf16)
        + each(lambda u: (2, 2, u, depth), bf16)
        + each(lambda u: (2, 2, u, depth), bf16)
        + each(lambda u: (NCH, 2, 4, 2, u, ch), f32)
        + each(lambda u: (NCH, 4, 2, u, ch), f32)
        + each(lambda u: (NCH, 2, u, ch), f32)
        + each(lambda u: (NCH, 2, 2, u, ch), f32)
        + each(lambda u: (2, u, rows), f32)
        + [
            pltpu.SemaphoreType.DMA((NCH,)),
            pltpu.SemaphoreType.DMA((R,)),
            pltpu.SemaphoreType.DMA((R, 2)),
            pltpu.SemaphoreType.DMA((R, 6)),
            pltpu.SemaphoreType.DMA((R, 6)),
            pltpu.SemaphoreType.DMA((R, 9)),
            pltpu.SemaphoreType.DMA((R, 9)),
            pltpu.SemaphoreType.DMA((R, NCH)),
            pltpu.SemaphoreType.DMA((R, NCH)),
            pltpu.SemaphoreType.DMA((R, NCH, 4)),
            pltpu.SemaphoreType.DMA((R, NCH, 4)),
        ]
    )
    result = pl.pallas_call(
        functools.partial(kernel, ROUNDS),
        name="ladder",
        out_shape=jax.ShapeDtypeStruct((2 * width, rows), f32),
        in_specs=[
            pl.BlockSpec(memory_space=pltpu.SMEM),
            pl.BlockSpec(memory_space=pl.ANY),
            pl.BlockSpec(memory_space=pl.ANY),
        ],
        out_specs=pl.BlockSpec(memory_space=pl.ANY),
        scratch_shapes=scratch,
        compiler_params=pltpu.CompilerParams(collective_id=0, has_side_effects=True, vmem_limit_bytes=66_500_000),
    )(block_owner, integrals, t2)
    return result.T


def solution(mesh):
    in_specs = (P("vv", "oo"), P(None, "oo", "vv"), P())
    return jax.shard_map(local, mesh=mesh, in_specs=in_specs, out_specs=P("vv", "oo"), check_vma=False)
```

```python
import functools

import jax
import jax.numpy as jnp
from jax import lax
from jax.experimental import pallas as pl
from jax.experimental.pallas import tpu as pltpu
from jax.sharding import PartitionSpec as P

MESH = pl.DeviceIdType.MESH
ROUNDS = (16, 16, 16, 16, 16)
NCH = 2
FULL = 32000.0
RHS_T = (((1,), (1,)), ((), ()))


def wrap(i):
    return lax.rem(i, 4)


def encode(ref, value):
    width = value.shape[-1]
    most = jnp.maximum(jnp.max(jnp.abs(value), axis=-1, keepdims=True), 1e-30)
    power = jnp.ceil(jnp.log2(most))
    scale = FULL * jnp.exp2(-power)
    ref[:, 0:width] = jnp.round(value * scale).astype(jnp.int16)
    ref[:, width : width + 128] = jnp.broadcast_to(power, (value.shape[0], 128)).astype(jnp.int16)


def decode(code):
    width = code.shape[-1] - 128
    power = code[:, width : width + 1].astype(jnp.float32)
    return code[:, 0:width].astype(jnp.float32) * (jnp.exp2(power) * (1.0 / FULL))


def kernel(rounds, owner, a_hbm, t_hbm, o_ref, *scratch):
    R = len(rounds)
    scratch = list(scratch)

    def take(n):
        got = scratch[:n]
        del scratch[:n]
        return got

    (a,) = take(1)
    t2v, snd, arr, fin, ra, rb, part, xin, q1, q2, yr, yin = (take(R) for _ in range(12))
    a_sem, t_sem, sA, rA, sB, rB, sX, rX, sY, rY = take(10)
    CH = a.shape[0] // NCH
    offs = [sum(rounds[:r]) for r in range(R)]

    v, o = lax.axis_index("vv"), lax.axis_index("oo")
    z, x, y, c = lax.div(v, 4), wrap(v), lax.div(o, 2), lax.rem(o, 2)
    f, s = z * (1 - c) + x * c, x * (1 - c) + z * c

    def plane(ff, ss):
        return ff * (4 - 3 * c) + ss * (1 + 3 * c)

    def dev_a(d):
        return (plane(wrap(f + d), s), o)

    def dev_b(d):
        return (plane(f, wrap(s + d)), o)

    def dev_y(d):
        return (v, wrap(y + d) * 2 + c)

    sibling = (v, y * 2 + 1 - c)

    def load_t(r):
        return pltpu.make_async_copy(t_hbm.at[:, pl.ds(offs[r], rounds[r]), :], t2v[r], t_sem.at[r])

    def load_a(i):
        rows = pl.ds(i * CH, CH)
        return pltpu.make_async_copy(a_hbm.at[rows], a.at[rows], a_sem.at[i])

    for r in range(R):
        load_t(r).start()
    for i in range(NCH):
        load_a(i).start()

    barrier = pltpu.get_barrier_semaphore()
    peers = [dev_a(1), dev_a(3), dev_b(1), dev_b(3), dev_y(1), dev_y(3), sibling]
    for peer in peers:
        pl.semaphore_signal(barrier, inc=1, device_id=peer, device_id_type=MESH)
    pl.semaphore_wait(barrier, len(peers))

    def send(src, dst, ss, rs, to):
        return pltpu.make_async_remote_copy(
            src_ref=src, dst_ref=dst, send_sem=ss, recv_sem=rs, device_id=to, device_id_type=MESH
        )

    def A(r, i):
        src, dst, d = [
            (snd[r].at[2, 0:2], ra[r].at[0], 1),
            (snd[r].at[2, 2:4], ra[r].at[1], 3),
            (snd[r].at[1], arr[r].at[1], 1),
            (snd[r].at[3], arr[r].at[3], 3),
            (ra[r].at[0], arr[r].at[2, 0:2], 1),
            (ra[r].at[1], arr[r].at[2, 2:4], 3),
        ][i]
        return send(src, dst, sA.at[r, i], rA.at[r, i], dev_a(d))

    def B(r, i):
        src, dst, d = [
            (snd[r].at[0, 2], rb[r].at[0, 0], 1),
            (snd[r].at[0, 1], fin[r].at[1, 0], 1),
            (snd[r].at[0, 3], fin[r].at[3, 0], 3),
            (arr[r].at[1, 2], rb[r].at[0, 1], 1),
            (arr[r].at[2:4, 2], rb[r].at[1], 3),
            (arr[r].at[1:4, 1], fin[r].at[1, 1:4], 1),
            (arr[r].at[1:4, 3], fin[r].at[3, 1:4], 3),
            (rb[r].at[0], fin[r].at[2, 0:2], 1),
            (rb[r].at[1], fin[r].at[2, 2:4], 3),
        ][i]
        return send(src, dst, sB.at[r, i], rB.at[r, i], dev_b(d))

    def X(r, ch):
        return send(part[r].at[ch, 1 - c], xin[r].at[ch], sX.at[r, ch], rX.at[r, ch], sibling)

    def Y(r, ch, i):
        src, dst, d = [
            (q1[r].at[ch, 0], yr[r].at[ch, 0], 1),
            (q1[r].at[ch, 1], yr[r].at[ch, 1], 3),
            (q2[r].at[ch, 0], yin[r].at[ch, 0], 1),
            (q2[r].at[ch, 1], yin[r].at[ch, 1], 3),
        ][i]
        return send(src, dst, sY.at[r, ch, i], rY.at[r, ch, i], dev_y(d))

    def prep(r):
        load_t(r).wait()
        for j in (2, 1, 3, 0):
            for t in range(4):
                block = t2v[r][owner[plane(wrap(f + j), wrap(s + t))]]
                if j == 0 and t == 0:
                    fin[r][0, 0] = block
                else:
                    snd[r][j, t] = block

    def multiply(r, ch):
        u = rounds[r]
        left = fin[r][...].reshape(16 * u, fin[r].shape[-1])
        rows = pl.ds(pl.multiple_of(ch * CH, CH), CH)
        res = lax.dot_general(left, a[rows, :], RHS_T, preferred_element_type=jnp.float32)
        for t in range(4):
            for j in range(4):
                ff, ss = wrap(f - j + 4), wrap(s - t + 4)
                zs, xs = ff * (1 - c) + ss * c, ss * (1 - c) + ff * c
                i = 4 * t + j
                part[r][ch, lax.div(xs, 2), zs, lax.rem(xs, 2)] = res[i * u : (i + 1) * u]
        X(r, ch).start()

    def chip_sum(r, ch):
        X(r, ch).wait_recv()
        part[r][ch, c] = part[r][ch, c] + xin[r][ch]
        far = part[r][ch, c, wrap(y + 2)]
        for h in range(2):
            encode(q1[r].at[ch, h], far[h])
        Y(r, ch, 0).start()
        Y(r, ch, 1).start()

    def compute(r):
        for i in (1, 2, 5, 6, 7, 8):
            B(r, i).wait_recv()
        for j in (1, 2, 3):
            fin[r][0, j] = arr[r][j, 0]
        if r == 0:
            for i in range(NCH):
                load_a(i).wait()

        multiply(r, 0)

        @pl.loop(1, NCH)
        def _(ch):
            multiply(r, ch)
            chip_sum(r, ch - 1)

        chip_sum(r, NCH - 1)

    def relay_y(r):
        @pl.loop(0, NCH)
        def _(ch):
            for i in range(2):
                d = wrap(y + 1 + 2 * i)
                near = part[r][ch, c, d]
                Y(r, ch, i).wait_recv()
                encode(q2[r].at[ch, i, i], near[i] + decode(yr[r][ch, i]))
                encode(q2[r].at[ch, i, 1 - i], near[1 - i])
                Y(r, ch, 2 + i).start()

    def finish(r):
        @pl.loop(0, NCH)
        def _(ch):
            Y(r, ch, 2).wait_recv()
            Y(r, ch, 3).wait_recv()
            cols = pl.ds(pl.multiple_of(ch * CH, CH), CH)
            for h in range(2):
                rows = pl.ds(80 * h + offs[r], rounds[r])
                o_ref[rows, cols] = part[r][ch, c, y, h] + decode(yin[r][ch, 0, h]) + decode(yin[r][ch, 1, h])

    prep(0)
    for k in range(-1, R + 3):
        if k + 1 < R:
            for i in range(4):
                A(k + 1, i).start()
            for i in range(3):
                B(k + 1, i).start()
        if k + 2 < R:
            prep(k + 2)
        if 0 <= k < R:
            for i in (2, 3, 4, 5):
                A(k, i).wait_recv()
            for i in (3, 4, 5, 6):
                B(k, i).start()
        if k + 1 < R:
            for i in range(2):
                A(k + 1, i).wait_recv()
                A(k + 1, 4 + i).start()
        if 0 <= k - 2 < R:
            relay_y(k - 2)
        if 0 <= k < R:
            B(k, 0).wait_recv()
            B(k, 3).wait_recv()
            B(k, 7).start()
            B(k, 4).wait_recv()
            B(k, 8).start()
        if 0 <= k - 3 < R:
            finish(k - 3)
        if 0 <= k - 1 < R:
            compute(k - 1)

    for r in range(R):
        for i in range(6):
            A(r, i).wait_send()
        for i in range(9):
            B(r, i).wait_send()

        @pl.loop(0, NCH)
        def _(ch):
            X(r, ch).wait_send()
            for i in range(4):
                Y(r, ch, i).wait_send()


def local(integrals, t2, block_owner):
    t2 = jnp.swapaxes(t2, 1, 2)
    groups, width, depth = t2.shape
    rows = integrals.shape[0]
    R, ch = len(ROUNDS), rows // NCH
    bf16, f32 = jnp.bfloat16, jnp.float32

    def each(shape, dtype):
        return [pltpu.VMEM(shape(u), dtype) for u in ROUNDS]

    scratch = (
        [pltpu.VMEM((rows, depth), bf16)]
        + each(lambda u: (groups, u, depth), bf16)
        + each(lambda u: (4, 4, u, depth), bf16)
        + each(lambda u: (4, 4, u, depth), bf16)
        + each(lambda u: (4, 4, u, depth), bf16)
        + each(lambda u: (2, 2, u, depth), bf16)
        + each(lambda u: (2, 2, u, depth), bf16)
        + each(lambda u: (NCH, 2, 4, 2, u, ch), f32)
        + each(lambda u: (NCH, 4, 2, u, ch), f32)
        + each(lambda u: (NCH, 2, u, ch + 128), jnp.int16)
        + each(lambda u: (NCH, 2, 2, u, ch + 128), jnp.int16)
        + each(lambda u: (NCH, 2, u, ch + 128), jnp.int16)
        + each(lambda u: (NCH, 2, 2, u, ch + 128), jnp.int16)
        + [
            pltpu.SemaphoreType.DMA((NCH,)),
            pltpu.SemaphoreType.DMA((R,)),
            pltpu.SemaphoreType.DMA((R, 6)),
            pltpu.SemaphoreType.DMA((R, 6)),
            pltpu.SemaphoreType.DMA((R, 9)),
            pltpu.SemaphoreType.DMA((R, 9)),
            pltpu.SemaphoreType.DMA((R, NCH)),
            pltpu.SemaphoreType.DMA((R, NCH)),
            pltpu.SemaphoreType.DMA((R, NCH, 4)),
            pltpu.SemaphoreType.DMA((R, NCH, 4)),
        ]
    )
    result = pl.pallas_call(
        functools.partial(kernel, ROUNDS),
        name="ladder",
        out_shape=pltpu.VMEM((2 * width, rows), f32),
        in_specs=[
            pl.BlockSpec(memory_space=pltpu.SMEM),
            pl.BlockSpec(memory_space=pl.ANY),
            pl.BlockSpec(memory_space=pl.ANY),
        ],
        out_specs=pl.BlockSpec(memory_space=pltpu.VMEM),
        scratch_shapes=scratch,
        compiler_params=pltpu.CompilerParams(collective_id=0, has_side_effects=True, vmem_limit_bytes=65_000_000),
    )(block_owner, integrals, t2)
    return result.T


def solution(mesh):
    in_specs = (P("vv", "oo"), P(None, "oo", "vv"), P())
    return jax.shard_map(local, mesh=mesh, in_specs=in_specs, out_specs=P("vv", "oo"), check_vma=False)
```

```python
import functools

import jax
import jax.numpy as jnp
from jax import lax
from jax.experimental import pallas as pl
from jax.experimental.pallas import tpu as pltpu
from jax.sharding import PartitionSpec as P

MESH = pl.DeviceIdType.MESH
ROUNDS = (24, 24, 16, 16)
NCH = 2
FULL = 32000.0
RHS_T = (((1,), (1,)), ((), ()))


def wrap(i):
    return lax.rem(i, 4)


def encode(ref, value):
    width = value.shape[-1]
    most = jnp.maximum(jnp.max(jnp.abs(value), axis=-1, keepdims=True), 1e-30)
    power = jnp.ceil(jnp.log2(most))
    scale = FULL * jnp.exp2(-power)
    ref[:, 0:width] = jnp.round(value * scale).astype(jnp.int16)
    ref[:, width : width + 128] = jnp.broadcast_to(power, (value.shape[0], 128)).astype(jnp.int16)


def decode(code):
    width = code.shape[-1] - 128
    power = code[:, width : width + 1].astype(jnp.float32)
    return code[:, 0:width].astype(jnp.float32) * (jnp.exp2(power) * (1.0 / FULL))


def kernel(rounds, owner, a_hbm, t_hbm, o_ref, *scratch):
    R = len(rounds)
    scratch = list(scratch)

    def take(n):
        got = scratch[:n]
        del scratch[:n]
        return got

    (a,) = take(1)
    t2v, snd, arr, fin, ra, rb, part, xin, q1, q2, yr, yin = (take(R) for _ in range(12))
    a_sem, t_sem, sA, rA, sB, rB, sX, rX, sY, rY = take(10)
    CH = a.shape[0] // NCH
    offs = [sum(rounds[:r]) for r in range(R)]

    v, o = lax.axis_index("vv"), lax.axis_index("oo")
    z, x, y, c = lax.div(v, 4), wrap(v), lax.div(o, 2), lax.rem(o, 2)
    f, s = z * (1 - c) + x * c, x * (1 - c) + z * c

    def plane(ff, ss):
        return ff * (4 - 3 * c) + ss * (1 + 3 * c)

    def dev_a(d):
        return (plane(wrap(f + d), s), o)

    def dev_b(d):
        return (plane(f, wrap(s + d)), o)

    def dev_y(d):
        return (v, wrap(y + d) * 2 + c)

    sibling = (v, y * 2 + 1 - c)

    def load_t(r):
        return pltpu.make_async_copy(t_hbm.at[:, pl.ds(offs[r], rounds[r]), :], t2v[r], t_sem.at[r])

    def load_a(i):
        rows = pl.ds(i * CH, CH)
        return pltpu.make_async_copy(a_hbm.at[rows], a.at[rows], a_sem.at[i])

    load_t(0).start()

    barrier = pltpu.get_barrier_semaphore()
    peers = [dev_a(1), dev_a(3), dev_b(1), dev_b(3), dev_y(1), dev_y(3), sibling]
    for peer in peers:
        pl.semaphore_signal(barrier, inc=1, device_id=peer, device_id_type=MESH)
    pl.semaphore_wait(barrier, len(peers))

    def send(src, dst, ss, rs, to):
        return pltpu.make_async_remote_copy(
            src_ref=src, dst_ref=dst, send_sem=ss, recv_sem=rs, device_id=to, device_id_type=MESH
        )

    def A(r, i):
        src, dst, d = [
            (snd[r].at[2, 0:2], ra[r].at[0], 1),
            (snd[r].at[2, 2:4], ra[r].at[1], 3),
            (snd[r].at[1], arr[r].at[1], 1),
            (snd[r].at[3], arr[r].at[3], 3),
            (ra[r].at[0], arr[r].at[2, 0:2], 1),
            (ra[r].at[1], arr[r].at[2, 2:4], 3),
        ][i]
        return send(src, dst, sA.at[r, i], rA.at[r, i], dev_a(d))

    def B(r, i):
        src, dst, d = [
            (snd[r].at[0, 2], rb[r].at[0, 0], 1),
            (snd[r].at[0, 1], fin[r].at[1, 0], 1),
            (snd[r].at[0, 3], fin[r].at[3, 0], 3),
            (arr[r].at[1, 2], rb[r].at[0, 1], 1),
            (arr[r].at[2:4, 2], rb[r].at[1], 3),
            (arr[r].at[1:4, 1], fin[r].at[1, 1:4], 1),
            (arr[r].at[1:4, 3], fin[r].at[3, 1:4], 3),
            (rb[r].at[0], fin[r].at[2, 0:2], 1),
            (rb[r].at[1], fin[r].at[2, 2:4], 3),
        ][i]
        return send(src, dst, sB.at[r, i], rB.at[r, i], dev_b(d))

    def X(r, ch):
        return send(part[r].at[ch, 1 - c], xin[r].at[ch], sX.at[r, ch], rX.at[r, ch], sibling)

    def Y(r, ch, i):
        src, dst, d = [
            (q1[r].at[ch, 0], yr[r].at[ch, 0], 1),
            (q1[r].at[ch, 1], yr[r].at[ch, 1], 3),
            (q2[r].at[ch, 0], yin[r].at[ch, 0], 1),
            (q2[r].at[ch, 1], yin[r].at[ch, 1], 3),
        ][i]
        return send(src, dst, sY.at[r, ch, i], rY.at[r, ch, i], dev_y(d))

    def prep(r):
        load_t(r).wait()
        for j in (2, 1, 3, 0):
            for t in range(4):
                block = t2v[r][owner[plane(wrap(f + j), wrap(s + t))]]
                if j == 0 and t == 0:
                    fin[r][0, 0] = block
                else:
                    snd[r][j, t] = block

    def multiply(r, ch):
        u = rounds[r]
        left = fin[r][...].reshape(16 * u, fin[r].shape[-1])
        rows = pl.ds(pl.multiple_of(ch * CH, CH), CH)
        res = lax.dot_general(left, a[rows, :], RHS_T, preferred_element_type=jnp.float32)
        for t in range(4):
            for j in range(4):
                ff, ss = wrap(f - j + 4), wrap(s - t + 4)
                zs, xs = ff * (1 - c) + ss * c, ss * (1 - c) + ff * c
                i = 4 * t + j
                part[r][ch, lax.div(xs, 2), zs, lax.rem(xs, 2)] = res[i * u : (i + 1) * u]
        X(r, ch).start()

    def chip_sum(r, ch):
        X(r, ch).wait_recv()
        part[r][ch, c] = part[r][ch, c] + xin[r][ch]
        far = part[r][ch, c, wrap(y + 2)]
        for h in range(2):
            encode(q1[r].at[ch, h], far[h])
        Y(r, ch, 0).start()
        Y(r, ch, 1).start()

    def compute(r):
        for i in (1, 2, 5, 6, 7, 8):
            B(r, i).wait_recv()
        for j in (1, 2, 3):
            fin[r][0, j] = arr[r][j, 0]
        if r == 0:
            for i in range(NCH):
                load_a(i).wait()

        multiply(r, 0)

        @pl.loop(1, NCH)
        def _(ch):
            multiply(r, ch)
            chip_sum(r, ch - 1)

        chip_sum(r, NCH - 1)

    def relay_y(r):
        @pl.loop(0, NCH)
        def _(ch):
            for i in range(2):
                d = wrap(y + 1 + 2 * i)
                near = part[r][ch, c, d]
                Y(r, ch, i).wait_recv()
                encode(q2[r].at[ch, i, i], near[i] + decode(yr[r][ch, i]))
                encode(q2[r].at[ch, i, 1 - i], near[1 - i])
                Y(r, ch, 2 + i).start()

    def finish(r):
        @pl.loop(0, NCH)
        def _(ch):
            Y(r, ch, 2).wait_recv()
            Y(r, ch, 3).wait_recv()
            cols = pl.ds(pl.multiple_of(ch * CH, CH), CH)
            for h in range(2):
                rows = pl.ds(80 * h + offs[r], rounds[r])
                o_ref[rows, cols] = part[r][ch, c, y, h] + decode(yin[r][ch, 0, h]) + decode(yin[r][ch, 1, h])

    prep(0)
    for k in range(-1, R + 3):
        if k + 1 < R:
            for i in range(4):
                A(k + 1, i).start()
            for i in range(3):
                B(k + 1, i).start()
        if k == -1:
            for r in range(1, R):
                load_t(r).start()
            for i in range(NCH):
                load_a(i).start()
        if k + 2 < R:
            prep(k + 2)
        if 0 <= k < R:
            for i in (2, 3, 4, 5):
                A(k, i).wait_recv()
            for i in (3, 4, 5, 6):
                B(k, i).start()
        if k + 1 < R:
            for i in range(2):
                A(k + 1, i).wait_recv()
                A(k + 1, 4 + i).start()
        if 0 <= k - 2 < R:
            relay_y(k - 2)
        if 0 <= k < R:
            B(k, 0).wait_recv()
            B(k, 3).wait_recv()
            B(k, 7).start()
            B(k, 4).wait_recv()
            B(k, 8).start()
        if 0 <= k - 3 < R:
            finish(k - 3)
        if 0 <= k - 1 < R:
            compute(k - 1)

    for r in range(R):
        for i in range(6):
            A(r, i).wait_send()
        for i in range(9):
            B(r, i).wait_send()

        @pl.loop(0, NCH)
        def _(ch):
            X(r, ch).wait_send()
            for i in range(4):
                Y(r, ch, i).wait_send()


def local(integrals, t2, block_owner):
    t2 = jnp.swapaxes(t2, 1, 2)
    groups, width, depth = t2.shape
    rows = integrals.shape[0]
    R, ch = len(ROUNDS), rows // NCH
    bf16, f32 = jnp.bfloat16, jnp.float32

    def each(shape, dtype):
        return [pltpu.VMEM(shape(u), dtype) for u in ROUNDS]

    scratch = (
        [pltpu.VMEM((rows, depth), bf16)]
        + each(lambda u: (groups, u, depth), bf16)
        + each(lambda u: (4, 4, u, depth), bf16)
        + each(lambda u: (4, 4, u, depth), bf16)
        + each(lambda u: (4, 4, u, depth), bf16)
        + each(lambda u: (2, 2, u, depth), bf16)
        + each(lambda u: (2, 2, u, depth), bf16)
        + each(lambda u: (NCH, 2, 4, 2, u, ch), f32)
        + each(lambda u: (NCH, 4, 2, u, ch), f32)
        + each(lambda u: (NCH, 2, u, ch + 128), jnp.int16)
        + each(lambda u: (NCH, 2, 2, u, ch + 128), jnp.int16)
        + each(lambda u: (NCH, 2, u, ch + 128), jnp.int16)
        + each(lambda u: (NCH, 2, 2, u, ch + 128), jnp.int16)
        + [
            pltpu.SemaphoreType.DMA((NCH,)),
            pltpu.SemaphoreType.DMA((R,)),
            pltpu.SemaphoreType.DMA((R, 6)),
            pltpu.SemaphoreType.DMA((R, 6)),
            pltpu.SemaphoreType.DMA((R, 9)),
            pltpu.SemaphoreType.DMA((R, 9)),
            pltpu.SemaphoreType.DMA((R, NCH)),
            pltpu.SemaphoreType.DMA((R, NCH)),
            pltpu.SemaphoreType.DMA((R, NCH, 4)),
            pltpu.SemaphoreType.DMA((R, NCH, 4)),
        ]
    )
    result = pl.pallas_call(
        functools.partial(kernel, ROUNDS),
        name="ladder",
        out_shape=pltpu.VMEM((2 * width, rows), f32),
        in_specs=[
            pl.BlockSpec(memory_space=pltpu.SMEM),
            pl.BlockSpec(memory_space=pl.ANY),
            pl.BlockSpec(memory_space=pl.ANY),
        ],
        out_specs=pl.BlockSpec(memory_space=pltpu.VMEM),
        scratch_shapes=scratch,
        compiler_params=pltpu.CompilerParams(collective_id=0, has_side_effects=True, vmem_limit_bytes=65_000_000),
    )(block_owner, integrals, t2)
    return result.T


def solution(mesh):
    in_specs = (P("vv", "oo"), P(None, "oo", "vv"), P())
    return jax.shard_map(local, mesh=mesh, in_specs=in_specs, out_specs=P("vv", "oo"), check_vma=False)
```
